32 devices in a mesh: dp: 16 (over z, y, x), tensor: 2 (over core).
Axes of the slice: x: 2, y: 2, z: 4, core: 2. Of those that a mesh axis runs over, the one named last changes fastest.
Arguments:
- inputs: bfloat16 [128, 196, 768], P(('dp', 'tensor')), may hold values from -6 to 6
- region: int32 [128, 196], P('dp'), may hold values from 0 to 3
- rel_index: int32 [49, 49], replicated, may hold values from 0 to 168, as said below
- w_qkv: bfloat16 [768, 3, 768], P('dp', None, 'tensor'), may hold values from -0.21875 to 0.21875
- w_out: bfloat16 [768, 768], P('dp', 'tensor'), may hold values from -0.75 to 0.75
- w_up: bfloat16 [768, 3072], P('dp', 'tensor'), may hold values from -0.21875 to 0.21875
- w_down: bfloat16 [768, 3072], P('dp', 'tensor'), may hold values from -0.15625 to 0.15625
- b_qv: float32 [2, 768], replicated, may hold values from -3 to 3
- bias_table: float32 [169, 24], replicated, may hold values from -4 to 300
- b_out: float32 [768], replicated, may hold values from -3 to 3
- b_up: float32 [3072], replicated, may hold values from -3 to 3
- b_down: float32 [768], replicated, may hold values from -3 to 3
- gain_one: float32 [768], replicated, may hold values from 0.25 to 1.75
- shift_one: float32 [768], replicated, may hold values from -3 to 3
- gain_two: float32 [768], replicated, may hold values from 0.25 to 1.75
- shift_two: float32 [768], replicated, may hold values from -3 to 3
- cotangent: bfloat16 [128, 196, 768], P(('dp', 'tensor')), may hold values from -6 to 6
Outputs:
- output: bfloat16 [128, 196, 768], P(('dp', 'tensor'))
- grad_inputs: float32 [128, 196, 768], P(('dp', 'tensor'))
- grad_w_qkv: float32 [768, 3, 768], P('dp', None, 'tensor')
- grad_w_out: float32 [768, 768], P('dp', 'tensor')
- grad_w_up: float32 [768, 3072], P('dp', 'tensor')
- grad_w_down: float32 [768, 3072], P('dp', 'tensor')
- grad_b_qv: float32 [2, 768], replicated
- grad_table: float32 [169, 24], replicated
- grad_b_out: float32 [768], replicated
- grad_b_up: float32 [3072], replicated
- grad_b_down: float32 [768], replicated
- grad_gain_one: float32 [768], replicated
- grad_shift_one: float32 [768], replicated
- grad_gain_two: float32 [768], replicated
- grad_shift_two: float32 [768], replicated
The draws below stay inside these ranges and needn't reach their ends.
Inputs may be any that keep to these rules, and one draw needn't show every extreme that they name: `rel_index`: each entry is the bias table row for the relative offset of query i and key j inside a window; equal offsets share a row and all 169 rows are used.
All inputs are finite; a program needn't handle non-finite values.
Results may differ from the reference program's by a relative error of at most 0.01.
Values may be sent and summed in bfloat16 or wider, within the bound.
No kernel may reach another device: no remote copies, remote signals or barrier semaphores. Data moves between devices by JAX's collectives and lax.ppermute only.
A program may use at most 192 MiB of HBM per device.

```python
import jax
import jax.numpy as jnp
from jax import lax

C = 768
HEADS = 24
HEAD_DIM = 32
FF = 3072
SIDE = 14
WIN = 7
SHIFT = 3
TOK_IMG = 196
TABLE = 169
IMAGES = 128
N_DP = 16


def relabel_of(key):
    return jax.random.permutation(jax.random.fold_in(key, 11), TABLE).astype(jnp.int32)


def draw_rel_index(key, part):
    relabel = relabel_of(key)
    window_cells = jnp.arange(WIN * WIN, dtype=jnp.int32)
    cell_rows = window_cells // WIN
    cell_cols = window_cells % WIN
    offset = (cell_rows[:, None] - cell_rows[None, :] + WIN - 1) * (2 * WIN - 1) + (cell_cols[:, None] - cell_cols[None, :] + WIN - 1)
    return relabel[offset]


def draw_bias_table(key, part):
    entries = jax.random.normal(jax.random.fold_in(key, 23), (TABLE, HEADS), jnp.float32)
    return jnp.clip(entries, -4.0, 4.0)


def set_ends(drawn, rng, smallest, top_value):
    extent = drawn.shape
    spot = [jax.random.randint(jax.random.fold_in(rng, axis), (), 0, extent[axis]) for axis in range(len(extent))]
    drawn = drawn.at[tuple(spot)].set(smallest)
    longest = extent.index(max(extent))
    spot[longest] = (spot[longest] + 1) % extent[longest]
    return drawn.at[tuple(spot)].set(top_value)


def raised(drawn, rng, source, target, blocks, factor):
    owner, partner = [(jnp.arange(drawn.shape[dim]) // (drawn.shape[dim] // blocks)).reshape([-1 if axis == dim else 1 for axis in range(drawn.ndim)]) for dim in (source, target)]
    chosen = jax.random.permutation(rng, blocks)[partner]
    strong = (owner == chosen) | (owner == (partner + blocks // 2) % blocks)
    return jnp.where(strong, factor * drawn, drawn)


def steps_of(key, shape, split, smallest, largest):
    def one(dim, shards_of):
        heights = jax.random.uniform(jax.random.fold_in(jax.random.fold_in(key, 6), dim), (shards_of,), jnp.float32, smallest / len(split), largest / len(split))
        return jnp.repeat(jnp.exp(heights), shape[dim] // shards_of).reshape((-1,) + (1,) * (len(shape) - dim - 1))

    gain = one(*split[0])
    for cut in split[1:]:
        gain = gain * one(*cut)
    return gain


def normal_values(stream_key, extent, width, reach, split=(), kind=jnp.bfloat16):
    loudness = steps_of(stream_key, extent, split, -0.22, 0.18) if split else 1.0
    values = jax.random.normal(stream_key, extent, jnp.float32) * width * loudness
    return jnp.minimum(jnp.maximum(values, -reach), reach).astype(kind)


def noise_with(own_key, dims, deviation, most, shards, heavy, held_as=jnp.bfloat16):
    array = deviation * jax.random.normal(own_key, dims, jnp.float32)
    if shards:
        array = array * steps_of(own_key, dims, shards, -0.22, 0.18)
    return jnp.clip(raised(array, jax.random.fold_in(own_key, 3), *heavy), -most, most).astype(held_as)


def setup_inputs(seed: int = 0) -> dict:
    key_of = jax.random.split(jax.random.key(seed), 18)
    return {
        "inputs": normal_values(key_of[0], (IMAGES, TOK_IMG, C), 1.0, 6.0, ((0, 32),)),
        "region": set_ends(jax.random.randint(key_of[1], (IMAGES, TOK_IMG), 0, 4), jax.random.fold_in(key_of[1], 1), 0, 3).astype(jnp.int32),
        "rel_index": draw_rel_index(jax.random.fold_in(key_of[17], 71), 0),
        "w_qkv": normal_values(key_of[3], (C, 3, C), C ** -0.5, 0.21875, ((0, 16), (2, 2))),
        "w_out": normal_values(key_of[4], (C, C), (C // 12) ** -0.5, 0.75, ((0, 16), (1, 2))),
        "w_up": normal_values(key_of[5], (C, FF), C ** -0.5, 0.21875, ((0, 16), (1, 2))),
        "w_down": normal_values(key_of[6], (C, FF), (FF // 2) ** -0.5, 0.15625, ((0, 16), (1, 2))),
        "b_qv": normal_values(key_of[7], (2, C), 0.5, 3.0, (), jnp.float32),
        "bias_table": draw_bias_table(jax.random.fold_in(key_of[17], 71), 0),
        "b_out": normal_values(key_of[9], (C,), 0.5, 3.0, (), jnp.float32),
        "b_up": normal_values(key_of[10], (FF,), 0.5, 3.0, (), jnp.float32),
        "b_down": normal_values(key_of[11], (C,), 0.5, 3.0, (), jnp.float32),
        "gain_one": jnp.clip(1.0 + 0.15 * jax.random.normal(key_of[12], (C,), jnp.float32), 0.25, 1.75),
        "shift_one": normal_values(key_of[13], (C,), 0.5, 3.0, (), jnp.float32),
        "gain_two": jnp.clip(1.0 + 0.15 * jax.random.normal(key_of[14], (C,), jnp.float32), 0.25, 1.75),
        "shift_two": normal_values(key_of[15], (C,), 0.5, 3.0, (), jnp.float32),
        "cotangent": noise_with(key_of[16], (IMAGES, TOK_IMG, C), 1.0, 6.0, ((0, 32),), (0, 2, 32, 2.75)),
    }


@jax.custom_vjp
def low(v):
    return lax.optimization_barrier(v.astype(jnp.bfloat16)).astype(jnp.float32)

@jax.custom_vjp
def low_back(v):
    return v

def low_keep(v):
    return (low(v), None)

def low_pass(kept, grad):
    return (grad,)

def back_keep(v):
    return (v, None)

def back_low(kept, grad):
    return (low(grad),)
low.defvjp(low_keep, low_pass)
low_back.defvjp(back_keep, back_low)
norm_eps = 1e-05

def layer_norm(values, norm_gain, norm_shift):
    average = lax.optimization_barrier(jnp.mean(values, axis=-1, keepdims=True))
    centred = values - average
    variance = lax.optimization_barrier(jnp.mean(centred * centred, axis=-1, keepdims=True))
    return centred * lax.rsqrt(variance + norm_eps) * norm_gain + norm_shift

def to_windows(tokens):
    batch_count = tokens.shape[0]
    trailing = tokens.shape[2:]
    across = SIDE // WIN
    lattice = tokens.reshape((batch_count, SIDE, SIDE) + trailing)
    lattice = jnp.roll(lattice, (-SHIFT, -SHIFT), axis=(1, 2))
    lattice = lattice.reshape((batch_count, across, WIN, across, WIN) + trailing)
    lattice = jnp.moveaxis(lattice, 3, 2)
    return lattice.reshape((batch_count * across * across, WIN * WIN) + trailing)

def from_windows(windows, batch_count):
    trailing = windows.shape[2:]
    across = SIDE // WIN
    lattice = windows.reshape((batch_count, across, across, WIN, WIN) + trailing)
    lattice = jnp.moveaxis(lattice, 2, 3)
    lattice = lattice.reshape((batch_count, SIDE, SIDE) + trailing)
    lattice = jnp.roll(lattice, (SHIFT, SHIFT), axis=(1, 2))
    return lattice.reshape((batch_count, SIDE * SIDE) + trailing)

def block_forward(params, inputs, region, rel_index):
    w_qkv, w_out, w_up, w_down, b_qv, bias_table, b_out, b_up, b_down, gain_one, shift_one, gain_two, shift_two = params
    highest = lax.Precision.HIGHEST
    batch_count = inputs.shape[0]
    normed_one = low(layer_norm(inputs, gain_one, shift_one))
    windows = to_windows(normed_one)
    labels = to_windows(region)
    window_count = windows.shape[0]
    qkv_mixed = jnp.einsum('wnc,cjd->wnjd', windows, w_qkv, precision=highest)
    scale_query = HEAD_DIM ** (-0.5)
    query_low = low(low_back(qkv_mixed[:, :, 0] + b_qv[0]) * scale_query)
    key_low = low(low_back(qkv_mixed[:, :, 1]))
    value_low = low(low_back(qkv_mixed[:, :, 2] + b_qv[1]))
    head_shape = (window_count, WIN * WIN, HEADS, HEAD_DIM)
    query_low = query_low.reshape(head_shape)
    key_low = key_low.reshape(head_shape)
    value_low = value_low.reshape(head_shape)
    scores = jnp.einsum('wqhd,wkhd->whqk', query_low, key_low, precision=highest)
    pair_bias = jnp.transpose(bias_table[rel_index], (2, 0, 1))
    masked = jnp.where(labels[:, :, None] == labels[:, None, :], 0.0, -100.0)
    scores = low_back(scores + pair_bias[None] + masked[:, None])
    attn_prob = low(jax.nn.softmax(scores, axis=-1))
    attended = jnp.einsum('whqk,wkhd->wqhd', attn_prob, value_low, precision=highest)
    attended = low(low_back(attended.reshape(window_count, WIN * WIN, C)))
    attended = from_windows(attended, batch_count)
    branch = low_back(jnp.einsum('ntc,oc->nto', attended, w_out, precision=highest) + b_out)
    middle = inputs + branch
    normed_two = low(layer_norm(middle, gain_two, shift_two))
    pre_act = low_back(jnp.einsum('ntc,cf->ntf', normed_two, w_up, precision=highest) + b_up)
    hidden = low(jax.nn.gelu(pre_act, approximate=False))
    return middle + (jnp.einsum('ntf,of->nto', hidden, w_down, precision=highest) + b_down)

def reference(inputs, region, rel_index, w_qkv, w_out, w_up, w_down, b_qv, bias_table, b_out, b_up, b_down, gain_one, shift_one, gain_two, shift_two, cotangent):
    params = tuple((item.astype(jnp.float32) for item in (w_qkv, w_out, w_up, w_down, b_qv, bias_table, b_out, b_up, b_down, gain_one, shift_one, gain_two, shift_two)))
    inputs_float = inputs.astype(jnp.float32)
    regions = region.reshape((N_DP, -1, TOK_IMG))

    def whole(params_in, inputs_in):
        blocked = inputs_in.reshape((N_DP, -1, TOK_IMG, C))
        step_fn = jax.checkpoint(lambda operands: block_forward(params_in, operands[0], operands[1], rel_index))
        results = lax.map(step_fn, (blocked, regions))
        return results.reshape(inputs_in.shape)
    result, pullback = jax.vjp(whole, params, inputs_float)
    grad_params, grad_inputs = pullback(cotangent.astype(jnp.float32))
    return (result.astype(jnp.bfloat16), grad_inputs, grad_params[0], grad_params[1], grad_params[2], grad_params[3], grad_params[4], grad_params[5], grad_params[6], grad_params[7], grad_params[8], grad_params[9], grad_params[10], grad_params[11], grad_params[12])
```

```python
import functools

import jax
import jax.numpy as jnp
from jax import lax
from jax.experimental import pallas as pl
from jax.experimental.pallas import tpu as pltpu
from jax.sharding import PartitionSpec as P

C = 768
HEADS = 24
HEAD_DIM = 32
FF = 3072
SIDE = 14
WIN = 7
SHIFT = 3
TABLE = 169

BF = jnp.bfloat16
F32 = jnp.float32
BOTH = ("dp", "tensor")

norm_eps = 1e-05
root_half = 0.7071067811865476
inv_root_tau = 0.3989422804014327


def first_pairs(n_dp):
    return [(d * 2 + t, (d ^ (1 << t)) * 2 + t) for d in range(n_dp) for t in range(2)]


def second_pairs(n_dp):
    return [(d * 2 + t, (d ^ (2 >> t)) * 2 + t) for d in range(n_dp) for t in range(2)]


def z_pairs(n_dp, s):
    return [(d * 2 + t, (d ^ (4 * s)) * 2 + t) for d in range(n_dp) for t in range(2)]


def core_pairs(n_dp):
    return [(d * 2 + t, d * 2 + 1 - t) for d in range(n_dp) for t in range(2)]


def send(value, pairs):
    return lax.ppermute(value, BOTH, pairs)


def gather_pieces(own, n_dp):
    nz = n_dp // 4
    column = jnp.stack([own] + [send(own, z_pairs(n_dp, s)) for s in range(1, nz)])
    a = send(column, first_pairs(n_dp))
    b = send(column, second_pairs(n_dp))
    c = send(a, second_pairs(n_dp))
    mine = [column, a, b, c]
    return mine + [send(v, core_pairs(n_dp)) for v in mine]


def slot_of(yx, core):
    y, x = yx // 2, yx % 2
    swapped = x * 2 + y
    return jnp.where(core == 0, y * 2 + x, swapped)


def assemble_kernel(parts, meta, *refs):
    pieces, outs = refs[:8], refs[8:]
    core, yx = meta[3], meta[0]
    for k in range(4):
        for half in range(2):
            whose = core if half == 0 else 1 - core
            rel = slot_of(jnp.int32(k), whose)
            place = rel ^ yx
            column = 0
            for out, (count, width) in zip(outs, parts):
                for j in range(count):
                    value = pieces[half * 4 + k][0, :, column : column + width]
                    column += width
                    left = pl.multiple_of(j * 2 * width + whose * width, 128)
                    out[0, place, :, pl.ds(left, width)] = value


def assemble(pieces, parts, meta):
    nz, rows, n = pieces[0].shape
    outs = [jax.ShapeDtypeStruct((nz, 4, rows, 2 * c * w), BF) for c, w in parts]
    got = pl.pallas_call(
        functools.partial(assemble_kernel, parts),
        grid_spec=pltpu.PrefetchScalarGridSpec(
            num_scalar_prefetch=1,
            grid=(nz,),
            in_specs=[pl.BlockSpec((1, rows, n), lambda s, m: (s, 0, 0))] * 8,
            out_specs=[
                pl.BlockSpec((1, 4, rows, 2 * c * w), lambda s, m: (s ^ m[1], 0, 0, 0))
                for c, w in parts
            ],
        ),
        out_shape=outs,
        name="assemble",
    )(meta, *pieces)
    return [g.reshape(nz * 4 * rows, -1) for g in got]


def scatter_kernel(parts, meta, *refs):
    grads, (own, other) = refs[: len(parts)], refs[len(parts) :]
    core, yx = meta[3], meta[0]
    for place in range(4):
        rel = jnp.int32(place) ^ yx
        for half, out in enumerate((own, other)):
            whose = core if half == 0 else 1 - core
            slot = slot_of(rel, whose)
            column = 0
            for grad, (count, width) in zip(grads, parts):
                for j in range(count):
                    left = pl.multiple_of(j * 2 * width + whose * width, 128)
                    out[slot, 0, :, column : column + width] = grad[
                        0, place, :, pl.ds(left, width)
                    ].astype(BF)
                    column += width


def split_grads(grads, parts, meta, n_dp):
    nz = n_dp // 4
    rows = C // n_dp
    n = sum(c * w for c, w in parts)
    grads = [g.reshape(nz, 4, rows, -1) for g in grads]
    return pl.pallas_call(
        functools.partial(scatter_kernel, parts),
        grid_spec=pltpu.PrefetchScalarGridSpec(
            num_scalar_prefetch=1,
            grid=(nz,),
            in_specs=[
                pl.BlockSpec((1, 4, rows, 2 * c * w), lambda s, m: (s ^ m[1], 0, 0, 0))
                for c, w in parts
            ],
            out_specs=[pl.BlockSpec((4, 1, rows, n), lambda s, m: (0, s, 0, 0))] * 2,
        ),
        out_shape=[jax.ShapeDtypeStruct((4, nz, rows, n), BF)] * 2,
        name="split_grads",
    )(meta, *grads)


def plus(a, b):
    return (a.astype(F32) + b.astype(F32)).astype(BF)


def reduce_grads(grads, parts, meta, n_dp):
    nz = n_dp // 4
    own, other = split_grads(grads, parts, meta, n_dp)
    total = plus(own, send(other, core_pairs(n_dp)))
    total = plus(total[:2], send(total[2:], second_pairs(n_dp)))
    total = plus(total[0], send(total[1], first_pairs(n_dp)))
    result = total[0].astype(F32)
    for s in range(1, nz):
        result = result + send(total[s], z_pairs(n_dp, s)).astype(F32)
    outs, column = [], 0
    for count, width in parts:
        outs.append(result[:, column : column + count * width])
        column += count * width
    return outs


def sum_everywhere(vec, n_dp):
    vec = vec + send(vec, core_pairs(n_dp))
    bit = 1
    while bit < n_dp:
        pairs = [(d * 2 + t, (d ^ bit) * 2 + t) for d in range(n_dp) for t in range(2)]
        vec = vec + send(vec, pairs)
        bit *= 2
    return vec


def norm_parts(values, norm_gain, norm_shift):
    average = jnp.mean(values, axis=-1, keepdims=True)
    centred = values - average
    variance = jnp.mean(centred * centred, axis=-1, keepdims=True)
    inverse = lax.rsqrt(variance + norm_eps)
    normal_hat = centred * inverse
    return (normal_hat * norm_gain + norm_shift, normal_hat, inverse)


def norm_back(grad_normed, normal_hat, inverse, norm_gain):
    scaled = grad_normed * norm_gain
    grad_values = inverse * (
        scaled
        - jnp.mean(scaled, axis=-1, keepdims=True)
        - normal_hat * jnp.mean(scaled * normal_hat, axis=-1, keepdims=True)
    )
    return (
        grad_values,
        jnp.sum(grad_normed * normal_hat, axis=(0, 1)),
        jnp.sum(grad_normed, axis=(0, 1)),
    )


def to_windows(tokens):
    batch_count = tokens.shape[0]
    trailing = tokens.shape[2:]
    across = SIDE // WIN
    lattice = tokens.reshape((batch_count, SIDE, SIDE) + trailing)
    lattice = jnp.roll(lattice, (-SHIFT, -SHIFT), axis=(1, 2))
    lattice = lattice.reshape((batch_count, across, WIN, across, WIN) + trailing)
    lattice = jnp.moveaxis(lattice, 3, 2)
    return lattice.reshape((batch_count * across * across, WIN * WIN) + trailing)


def from_windows(windows, batch_count):
    trailing = windows.shape[2:]
    across = SIDE // WIN
    lattice = windows.reshape((batch_count, across, across, WIN, WIN) + trailing)
    lattice = jnp.moveaxis(lattice, 2, 3)
    lattice = lattice.reshape((batch_count, SIDE, SIDE) + trailing)
    lattice = jnp.roll(lattice, (SHIFT, SHIFT), axis=(1, 2))
    return lattice.reshape((batch_count, SIDE * SIDE) + trailing)


def body(
    n_dp,
    inputs,
    region,
    rel_index,
    w_qkv,
    w_out,
    w_up,
    w_down,
    b_qv,
    bias_table,
    b_out,
    b_up,
    b_down,
    gain_one,
    shift_one,
    gain_two,
    shift_two,
    cotangent,
):
    highest = lax.Precision.HIGHEST
    piece_qkv, piece_out, piece_up, piece_down = (w_qkv, w_out, w_up, w_down)
    dp, core = lax.axis_index("dp"), lax.axis_index("tensor")
    meta = jnp.stack([dp % 4, dp // 4, dp, core]).astype(jnp.int32)
    rows = C // n_dp
    half = C // 2
    parts_a, parts_b, parts_c = [(3, half)], [(1, half), (1, FF // 2)], [(1, FF // 2)]
    pieces_a = gather_pieces(piece_qkv.reshape(rows, -1), n_dp)
    pieces_b = gather_pieces(jnp.concatenate([piece_out, piece_up], axis=1), n_dp)
    pieces_c = gather_pieces(piece_down, n_dp)
    (full_qkv,) = assemble(pieces_a, parts_a, meta)
    full_qkv = full_qkv.reshape(C, 3, C)
    full_out, full_up = assemble(pieces_b, parts_b, meta)
    (full_down,) = assemble(pieces_c, parts_c, meta)
    back_qkv, back_out, back_up, back_down = full_qkv, full_out, full_up, full_down
    local_width = full_out.shape[1]
    local_hidden = full_up.shape[1]
    local_heads = local_width // HEAD_DIM
    scale_query = HEAD_DIM ** (-0.5)
    bias_qv, bias_up, table_local = b_qv, b_up, bias_table
    region = lax.dynamic_slice_in_dim(region, core * inputs.shape[0], inputs.shape[0], 0)
    pair_count = WIN * WIN
    offsets = lax.broadcasted_iota(jnp.int32, (pair_count * pair_count, TABLE), 1)
    onehot = (rel_index.reshape(-1, 1) == offsets).astype(jnp.float32)
    pair_bias = jnp.dot(onehot, table_local, precision=highest)
    pair_bias = jnp.transpose(pair_bias.reshape(pair_count, pair_count, local_heads), (2, 0, 1))
    inputs_float = inputs.astype(jnp.float32)
    normed_one, hat_one, inverse_one = norm_parts(inputs_float, gain_one, shift_one)
    group_one = normed_one.astype(BF)
    images = group_one.shape[0]
    labels = to_windows(region)
    masked = jnp.where(labels[:, :, None] == labels[:, None, :], 0.0, -100.0).astype(jnp.float32)
    windows = to_windows(group_one)
    window_count = windows.shape[0]
    head_shape = (window_count, pair_count, local_heads, HEAD_DIM)
    qkv_mixed = jnp.einsum("wnc,cjd->wnjd", windows, full_qkv, preferred_element_type=jnp.float32)
    query_low = (
        ((qkv_mixed[:, :, 0] + bias_qv[0]) * scale_query).astype(jnp.bfloat16).reshape(head_shape)
    )
    key_low = qkv_mixed[:, :, 1].astype(jnp.bfloat16).reshape(head_shape)
    value_low = (qkv_mixed[:, :, 2] + bias_qv[1]).astype(jnp.bfloat16).reshape(head_shape)

    def score_of():
        raw = jnp.einsum("wqhd,wkhd->whqk", query_low, key_low, preferred_element_type=jnp.float32)
        return raw + pair_bias[None] + masked[:, None]

    scores = score_of()
    row_peak = jnp.max(scores, axis=-1, keepdims=True)
    row_total = jnp.sum(jnp.exp(scores - row_peak), axis=-1, keepdims=True)
    logsum = row_peak + jnp.log(row_total)
    attn_prob = jnp.exp(scores - logsum).astype(jnp.bfloat16)
    attended = jnp.einsum(
        "whqk,wkhd->wqhd", attn_prob, value_low, preferred_element_type=jnp.float32
    )
    attended = attended.astype(jnp.bfloat16).reshape(window_count, pair_count, local_width)
    attended_tokens = from_windows(attended, images)
    partial_value = jnp.einsum(
        "ntc,oc->nto", attended_tokens, full_out, preferred_element_type=jnp.float32
    )
    branch_sum = partial_value
    middle = inputs_float + (branch_sum + b_out)
    normed_two, hat_two, inverse_two = norm_parts(middle, gain_two, shift_two)
    group_two = normed_two.astype(BF)
    pre_act = (
        jnp.einsum("ntc,cf->ntf", group_two, full_up, preferred_element_type=jnp.float32) + bias_up
    )
    hidden = jax.nn.gelu(pre_act, approximate=False).astype(jnp.bfloat16)
    partial_mlp = jnp.einsum("ntf,of->nto", hidden, full_down, preferred_element_type=jnp.float32)
    mlp_sum = partial_mlp
    output = middle + (mlp_sum + b_down)
    grad_output = cotangent.astype(jnp.float32)
    grad_bias_down = jnp.sum(grad_output, axis=(0, 1))
    group_grad = cotangent
    grad_down = jnp.einsum("nto,ntf->of", group_grad, hidden, preferred_element_type=jnp.float32)
    grad_hidden = jnp.einsum(
        "nto,of->ntf", group_grad, back_down, preferred_element_type=jnp.float32
    )
    gelu_slope = (
        0.5 * (1.0 + lax.erf(pre_act * root_half))
        + pre_act * jnp.exp(-0.5 * pre_act * pre_act) * inv_root_tau
    )
    grad_pre = (grad_hidden * gelu_slope).astype(jnp.bfloat16)
    grad_bias_up = jnp.sum(grad_pre, axis=(0, 1), dtype=jnp.float32)
    grad_up = jnp.einsum("ntc,ntf->cf", group_two, grad_pre, preferred_element_type=jnp.float32)
    partial_two = jnp.einsum("ntf,cf->ntc", grad_pre, back_up, preferred_element_type=jnp.float32)
    grad_normed_two = partial_two
    grad_middle_norm, grad_gain_two, grad_shift_two = norm_back(
        grad_normed_two, hat_two, inverse_two, gain_two
    )
    grad_middle = grad_output + grad_middle_norm
    grad_branch = grad_middle.astype(jnp.bfloat16)
    grad_bias_out = jnp.sum(grad_branch, axis=(0, 1), dtype=jnp.float32)
    group_branch = grad_branch
    grad_wout = jnp.einsum(
        "nto,ntc->oc", group_branch, attended_tokens, preferred_element_type=jnp.float32
    )
    grad_attended = jnp.einsum(
        "nto,oc->ntc", group_branch, back_out, preferred_element_type=jnp.float32
    )
    grad_attended = to_windows(grad_attended.astype(jnp.bfloat16)).reshape(head_shape)
    prob_again = jnp.exp(score_of() - logsum)
    grad_value = jnp.einsum(
        "whqk,wqhd->wkhd",
        prob_again.astype(jnp.bfloat16),
        grad_attended,
        preferred_element_type=jnp.float32,
    )
    grad_prob = jnp.einsum(
        "wqhd,wkhd->whqk", grad_attended, value_low, preferred_element_type=jnp.float32
    )
    grad_scores = prob_again * (grad_prob - jnp.sum(prob_again * grad_prob, axis=-1, keepdims=True))
    grad_scores = grad_scores.astype(jnp.bfloat16)
    pair_grad = jnp.sum(grad_scores, axis=0, dtype=jnp.float32)
    pair_grad = jnp.transpose(pair_grad, (1, 2, 0)).reshape(pair_count * pair_count, local_heads)
    table_grad_local = jnp.dot(onehot.T, pair_grad, precision=highest)
    table_grad = table_grad_local
    grad_query = (
        jnp.einsum("whqk,wkhd->wqhd", grad_scores, key_low, preferred_element_type=jnp.float32)
        * scale_query
    ).astype(jnp.bfloat16)
    grad_key = jnp.einsum(
        "whqk,wqhd->wkhd", grad_scores, query_low, preferred_element_type=jnp.float32
    ).astype(jnp.bfloat16)
    grad_value = grad_value.astype(jnp.bfloat16)
    grad_mixed = jnp.stack([grad_query, grad_key, grad_value], axis=2)
    grad_mixed = from_windows(grad_mixed.reshape(window_count, pair_count, 3, local_width), images)
    grad_bias_qv = jnp.sum(grad_mixed[:, :, 0::2], axis=(0, 1), dtype=jnp.float32)
    grad_qkv = jnp.einsum(
        "ntc,ntjd->cjd", group_one, grad_mixed, preferred_element_type=jnp.float32
    )
    partial_one = jnp.einsum(
        "ntjd,cjd->ntc", grad_mixed, back_qkv, preferred_element_type=jnp.float32
    )
    grad_normed_one = partial_one
    grad_input_norm, grad_gain_one, grad_shift_one = norm_back(
        grad_normed_one, hat_one, inverse_one, gain_one
    )
    grad_inputs = grad_middle + grad_input_norm
    (shard_down,) = reduce_grads([grad_down], parts_c, meta, n_dp)
    (shard_up,) = reduce_grads([grad_up], parts_c, meta, n_dp)
    shard_out, shard_qkv = reduce_grads(
        [grad_wout, grad_qkv.reshape(C, 3 * C)], [(1, half), (3, half)], meta, n_dp
    )
    shard_qkv = shard_qkv.reshape(rows, 3, half)
    small = (
        grad_bias_qv,
        table_grad,
        grad_bias_out,
        grad_bias_up,
        grad_bias_down,
        grad_gain_one,
        grad_shift_one,
        grad_gain_two,
        grad_shift_two,
    )
    flat = jnp.concatenate([v.reshape(-1) for v in small])
    pad = -flat.shape[0] % 1024
    flat = sum_everywhere(jnp.pad(flat, (0, pad)).reshape(-1, 128), n_dp).reshape(-1)
    summed, start = [], 0
    for v in small:
        summed.append(flat[start : start + v.size].reshape(v.shape))
        start += v.size
    return (
        output.astype(jnp.bfloat16),
        grad_inputs,
        shard_qkv,
        shard_out,
        shard_up,
        shard_down,
        summed[0],
        summed[1],
        summed[2],
        summed[3],
        summed[4],
        summed[5],
        summed[6],
        summed[7],
        summed[8],
    )


def solution(mesh):
    placed = (
        P(("dp", "tensor"), None, None),
        P("dp", None),
        P(),
        P("dp", None, "tensor"),
        P("dp", "tensor"),
        P("dp", "tensor"),
        P("dp", "tensor"),
        P(),
        P(),
        P(),
        P(),
        P(),
        P(),
        P(),
        P(),
        P(),
        P(("dp", "tensor"), None, None),
    )
    return jax.shard_map(
        functools.partial(body, mesh.shape["dp"]),
        mesh=mesh,
        in_specs=placed,
        out_specs=(
            P(("dp", "tensor"), None, None),
            P(("dp", "tensor"), None, None),
            P("dp", None, "tensor"),
            P("dp", "tensor"),
            P("dp", "tensor"),
            P("dp", "tensor"),
            P(),
            P(),
            P(),
            P(),
            P(),
            P(),
            P(),
            P(),
            P(),
        ),
        check_vma=False,
    )
```

```python
import functools

import jax
import jax.numpy as jnp
import numpy as np
from jax import lax
from jax.experimental import pallas as pl
from jax.experimental.pallas import tpu as pltpu
from jax.sharding import PartitionSpec as P

C = 768
HALF = 384
HEADS = 24
HEAD_DIM = 32
FF = 3072
SIDE = 14
WIN = 7
SHIFT = 3
TABLE = 169
TOK_IMG = SIDE * SIDE
NAT = 208
PAIR = 112
UNITS = 3
CHUNK = 768
BLOCKS = 16
ROWS = C // BLOCKS
FAR = -1e30

BF = jnp.bfloat16
F32 = jnp.float32
BOTH = ("dp", "tensor")

norm_eps = 1e-05
root_half = 0.7071067811865476
inv_root_tau = 0.3989422804014327


def first_pairs(n_dp):
    return [(d * 2 + t, (d ^ (1 << t)) * 2 + t) for d in range(n_dp) for t in range(2)]


def second_pairs(n_dp):
    return [(d * 2 + t, (d ^ (2 >> t)) * 2 + t) for d in range(n_dp) for t in range(2)]


def z_pairs(n_dp, s):
    return [(d * 2 + t, (d ^ (4 * s)) * 2 + t) for d in range(n_dp) for t in range(2)]


def core_pairs(n_dp):
    return [(d * 2 + t, d * 2 + 1 - t) for d in range(n_dp) for t in range(2)]


def send(value, pairs):
    return lax.ppermute(value, BOTH, pairs)


def staged(n_dp):
    return n_dp == BLOCKS


def gather_pieces(own, n_dp):
    if not staged(n_dp):
        full = lax.all_gather(own, "dp", axis=0, tiled=True)
        halves = (full, send(full, core_pairs(n_dp)))
        blocks = [h.reshape(BLOCKS // 4, 4, ROWS, -1) for h in halves]
        return [[b[:, k] for k in range(4)] for b in blocks]
    column = jnp.stack([own] + [send(own, z_pairs(n_dp, s)) for s in range(1, 4)])
    a = send(column, first_pairs(n_dp))
    b = send(column, second_pairs(n_dp))
    c = send(a, second_pairs(n_dp))
    mine = [column, a, b, c]
    return [mine, [send(v, core_pairs(n_dp)) for v in mine]]


def plus(a, b):
    return (a.astype(F32) + b.astype(F32)).astype(BF)


def reduce_blocks(own, other, n_dp):
    total = plus(own, send(other, core_pairs(n_dp)))
    if not staged(n_dp):
        full = total.transpose(1, 0, 2, 3).reshape(C, -1).astype(F32)
        return lax.psum_scatter(full, "dp", scatter_dimension=0, tiled=True)
    total = plus(total[:2], send(total[2:], second_pairs(n_dp)))
    total = plus(total[0], send(total[1], first_pairs(n_dp)))
    result = total[0].astype(F32)
    for s in range(1, 4):
        result = result + send(total[s], z_pairs(n_dp, s)).astype(F32)
    return result


def sum_everywhere(vec, n_dp):
    vec = vec + send(vec, core_pairs(n_dp))
    bit = 1
    while bit < n_dp:
        pairs = [(d * 2 + t, (d ^ bit) * 2 + t) for d in range(n_dp) for t in range(2)]
        vec = vec + send(vec, pairs)
        bit *= 2
    return vec


def dot(a, b):
    return lax.dot_general(a, b, (((1,), (0,)), ((), ())), preferred_element_type=F32)


def dot_t(a, b):
    return lax.dot_general(a, b, (((1,), (1,)), ((), ())), preferred_element_type=F32)


def unit_matrix(n):
    rows = lax.broadcasted_iota(jnp.int32, (n, n), 0)
    columns = lax.broadcasted_iota(jnp.int32, (n, n), 1)
    return jnp.where(rows == columns, 1.0, 0.0).astype(F32).astype(BF)


def slot_of(yx, whose):
    y, x = yx // 2, yx % 2
    return jnp.where(whose == 0, yx, x * 2 + y)


def piece_copies(pieces, whose, meta, columns, target, sem, base=0):
    copies = []
    for k, piece in enumerate(pieces):
        place = slot_of(jnp.int32(k), whose) ^ meta[0]
        for s in range(BLOCKS // 4):
            block = (jnp.int32(s) ^ meta[1]) * 4 + place
            row = pl.multiple_of(block * ROWS + base, 16)
            copies.append(
                pltpu.make_async_copy(
                    piece.at[s, :, columns], target.at[pl.ds(row, ROWS), :], sem
                )
            )
    return copies


def store_blocks(out, value, whose, meta, column, width):
    for block in range(BLOCKS):
        slot = slot_of(jnp.int32(block % 4) ^ meta[0], whose)
        z = jnp.int32(block // 4) ^ meta[1]
        out[slot, z, :, pl.ds(column, width)] = value[block * ROWS : (block + 1) * ROWS].astype(BF)


def norm_stats(v):
    mean = jnp.sum(v, axis=-1, keepdims=True) * (1.0 / C)
    centred = v - mean
    inverse = lax.rsqrt(jnp.sum(centred * centred, axis=-1, keepdims=True) * (1.0 / C) + norm_eps)
    return centred * inverse, inverse


def norm_back(grad, hat, inverse, gain):
    scaled = grad * gain
    mean = jnp.sum(scaled, axis=-1, keepdims=True) * (1.0 / C)
    cross = jnp.sum(scaled * hat, axis=-1, keepdims=True) * (1.0 / C)
    return inverse * (scaled - mean - hat * cross)


def transpose_into(out, ref):
    eye = unit_matrix(256)

    def step(j, carry):
        columns = pl.ds(pl.multiple_of(j * 256, 256), 256)
        out[columns, :] = dot_t(eye, ref[:, columns]).astype(BF)
        return carry

    lax.fori_loop(0, C // 256, step, 0)


def prologue_kernel(x, gy, gain, shift, to_window, n1, n1w, n1t, gyt, gbd, acc):
    i = pl.program_id(0)
    rows = pl.ds(pl.multiple_of(i * NAT, 16), NAT)
    hat, _ = norm_stats(x[...].astype(F32))
    normed = (hat * gain[...] + shift[...]).astype(BF)
    n1[rows, :] = normed
    acc[rows, :] = gy[...]
    for p in range(2):
        n1w[p * PAIR : (p + 1) * PAIR, :] = dot(to_window[p], normed).astype(BF)
    part = jnp.sum(gy[...].astype(F32), axis=0, keepdims=True)

    @pl.when(i == 0)
    def _():
        gbd[...] = part

    @pl.when(i > 0)
    def _():
        gbd[...] += part

    @pl.when(i == pl.num_programs(0) - 1)
    def _():
        transpose_into(n1t, n1)
        transpose_into(gyt, acc)


def whole(shape):
    return pl.BlockSpec(shape, lambda *a: (0,) * len(shape))


def anywhere(n):
    return [pl.BlockSpec(memory_space=pl.ANY)] * n


def params(flops, moved, **more):
    return dict(
        cost_estimate=pl.CostEstimate(flops=flops, bytes_accessed=moved, transcendentals=0),
        compiler_params=pltpu.CompilerParams(vmem_limit_bytes=60 * 2**20, **more),
    )


def prologue(x, gy, gain, shift, to_window):
    images = x.shape[0] // NAT
    t, tw = images * NAT, images * 2 * PAIR
    return pl.pallas_call(
        prologue_kernel,
        grid=(images,),
        in_specs=[
            pl.BlockSpec((NAT, C), lambda i: (i, 0)),
            pl.BlockSpec((NAT, C), lambda i: (i, 0)),
            whole((1, C)),
            whole((1, C)),
            whole((2, PAIR, NAT)),
        ],
        out_specs=[
            whole((t, C)),
            pl.BlockSpec((2 * PAIR, C), lambda i: (i, 0)),
            whole((C, t)),
            whole((C, t)),
            whole((1, C)),
        ],
        out_shape=[
            jax.ShapeDtypeStruct((t, C), BF),
            jax.ShapeDtypeStruct((tw, C), BF),
            jax.ShapeDtypeStruct((C, t), BF),
            jax.ShapeDtypeStruct((C, t), BF),
            jax.ShapeDtypeStruct((1, C), F32),
        ],
        scratch_shapes=[pltpu.VMEM((t, C), BF)],
        name="prologue",
        **params(10**9, 8 * 2**20),
    )(x, gy, gain, shift, to_window)


def attend_kernel(meta, n1w, bias_row, scale_row, bias, regm, lanes, to_nat, *refs):
    pieces, (att, qkv, probs), (weight, sem) = refs[:4], refs[4:7], refs[7:]
    i = pl.program_id(0)

    @pl.when(i == 0)
    def _():
        copies = piece_copies(pieces, meta[2], meta, pl.ds(0, 3 * HALF), weight, sem)
        for copy in copies:
            copy.start()
        for copy in copies:
            copy.wait()

        def step(j, carry):
            columns = pl.ds(pl.multiple_of(j * HALF, 128), HALF)
            value = dot(n1w[...], weight[:, columns]) + bias_row[:, columns]
            qkv[:, columns] = (value * scale_row[:, columns]).astype(BF)
            return carry

        lax.fori_loop(0, 3, step, 0)

    eye = unit_matrix(128)
    total = jnp.zeros((NAT, HALF), F32)
    for p in range(2):
        rows = pl.ds(pl.multiple_of((i * 2 + p) * PAIR, 16), PAIR)
        mask = regm[p]
        outs = []
        for u in range(UNITS):
            q = qkv[rows, u * 128 : (u + 1) * 128]
            k = qkv[rows, HALF + u * 128 : HALF + (u + 1) * 128]
            v = qkv[rows, 2 * HALF + u * 128 : 2 * HALF + (u + 1) * 128]
            stacked = jnp.concatenate([k * lanes[h : h + 1, :] for h in range(4)], axis=0)
            s = dot_t(stacked, q) + bias[u]
            s = s.reshape(4, PAIR, PAIR) + mask[None]
            e = jnp.exp(s - jnp.max(s, axis=1, keepdims=True))
            low = (e * (1.0 / jnp.sum(e, axis=1, keepdims=True))).astype(BF)
            probs[p, u] = low.reshape(4 * PAIR, PAIR)
            vt = dot_t(eye, v).astype(BF)
            for h in range(4):
                outs.append(dot(vt[h * 32 : (h + 1) * 32], low[h]).astype(BF))
        total = total + dot_t(to_nat[p], jnp.concatenate(outs, axis=0))
    att[...] = total.astype(BF)


def attend(meta, n1w, bias_row, scale_row, bias, regm, lanes, to_nat, pieces):
    images = n1w.shape[0] // (2 * PAIR)
    t, tw = images * NAT, images * 2 * PAIR
    return pl.pallas_call(
        attend_kernel,
        grid_spec=pltpu.PrefetchScalarGridSpec(
            num_scalar_prefetch=1,
            grid=(images,),
            in_specs=[
                whole((tw, C)),
                whole((1, 3 * HALF)),
                whole((1, 3 * HALF)),
                pl.BlockSpec((UNITS, 4 * PAIR, PAIR), lambda i, m: (m[2], 0, 0)),
                pl.BlockSpec((2, PAIR, PAIR), lambda i, m: (i, 0, 0)),
                whole((8, 128)),
                whole((2, NAT, PAIR)),
                *anywhere(4),
            ],
            out_specs=[
                pl.BlockSpec((NAT, HALF), lambda i, m: (i, 0)),
                whole((tw, 3 * HALF)),
                pl.BlockSpec((2, UNITS, 4 * PAIR, PAIR), lambda i, m: (i, 0, 0, 0)),
            ],
            scratch_shapes=[pltpu.VMEM((C, 3 * HALF), BF), pltpu.SemaphoreType.DMA],
        ),
        out_shape=[
            jax.ShapeDtypeStruct((t, HALF), BF),
            jax.ShapeDtypeStruct((tw, 3 * HALF), BF),
            jax.ShapeDtypeStruct((2 * images, UNITS, 4 * PAIR, PAIR), BF),
        ],
        name="attend",
        **params(4 * 10**9, 10 * 2**20),
    )(meta, n1w, bias_row, scale_row, bias, regm, lanes, to_nat, *pieces)


def middle_kernel(off, meta, x, att_own, att_par, b_out, gain, shift, *refs):
    own, par = refs[:4], refs[4:8]
    middle, n2, n2t, w_own, w_par, sem = refs[8:]
    columns = pl.ds(off, HALF)
    copies = piece_copies(own, meta[2], meta, columns, w_own, sem)
    copies += piece_copies(par, 1 - meta[2], meta, columns, w_par, sem)
    for copy in copies:
        copy.start()
    for copy in copies:
        copy.wait()
    images = x.shape[0] // NAT

    def step(i, carry):
        rows = pl.ds(pl.multiple_of(i * NAT, 16), NAT)
        branch = dot_t(att_own[rows, :], w_own[...]) + dot_t(att_par[rows, :], w_par[...])
        value = x[rows, :].astype(F32) + (branch + b_out[...])
        middle[rows, :] = value
        hat, _ = norm_stats(value)
        n2[rows, :] = (hat * gain[...] + shift[...]).astype(BF)
        return carry

    lax.fori_loop(0, images, step, 0)
    transpose_into(n2t, n2)


def middle_forward(off, meta, x, att_own, att_par, b_out, gain, shift, own, par):
    t = x.shape[0]
    return pl.pallas_call(
        functools.partial(middle_kernel, off),
        grid_spec=pltpu.PrefetchScalarGridSpec(
            num_scalar_prefetch=1,
            grid=(1,),
            in_specs=[
                whole((t, C)),
                whole((t, HALF)),
                whole((t, HALF)),
                whole((1, C)),
                whole((1, C)),
                whole((1, C)),
                *anywhere(8),
            ],
            out_specs=[whole((t, C)), whole((t, C)), whole((C, t))],
            scratch_shapes=[
                pltpu.VMEM((C, HALF), BF),
                pltpu.VMEM((C, HALF), BF),
                pltpu.SemaphoreType.DMA,
            ],
        ),
        out_shape=[
            jax.ShapeDtypeStruct((t, C), F32),
            jax.ShapeDtypeStruct((t, C), BF),
            jax.ShapeDtypeStruct((C, t), BF),
        ],
        name="middle_forward",
        **params(10**9, 9 * 2**20),
    )(meta, x, att_own, att_par, b_out, gain, shift, *own, *par)


def feed_kernel(offs, first, meta, n2, n2t, gy, gyt, bu, *refs):
    pieces = (refs[:4], refs[4:8])
    refs = refs[8:]
    if not first:
        out_in, gn_in, refs = refs[0], refs[1], refs[2:]
    dw_own, dw_par, out, gn, gbu, wu, wd, pre, gh, hid, gp, sems = refs
    t = n2.shape[0]
    all_copies = []
    for half in range(2):
        whose = meta[2] if half == 1 else 1 - meta[2]
        part = pieces[1 - half]
        all_copies.append(
            piece_copies(part, whose, meta, pl.ds(offs[0], CHUNK), wu.at[half], sems.at[half])
            + piece_copies(part, whose, meta, pl.ds(offs[1], CHUNK), wd.at[half], sems.at[half])
        )
    for copies in all_copies:
        for copy in copies:
            copy.start()
    for half in range(2):
        whose = meta[2] if half == 1 else 1 - meta[2]
        dw = dw_own if half == 1 else dw_par
        for copy in all_copies[half]:
            copy.wait()

        def tile(j, carry):
            columns = pl.ds(pl.multiple_of(j * 256, 256), 256)
            wu_t, wd_t = wu[half, :, columns], wd[half, :, columns]
            pre[...] = dot(n2[...], wu_t)
            gh[...] = dot(gy[...], wd_t)
            b = bu[half : half + 1, columns]

            def part(r, total):
                rows = pl.ds(pl.multiple_of(r * 64, 64), 64)
                u = pre[rows, :] + b
                phi = 0.5 * (1.0 + lax.erf(u * root_half))
                slope = phi + u * jnp.exp(-0.5 * u * u) * inv_root_tau
                grad = (gh[rows, :] * slope).astype(BF)
                hid[rows, columns] = (u * phi).astype(BF)
                gp[rows, columns] = grad
                return total + jnp.sum(grad.astype(F32), axis=0, keepdims=True)

            gbu[half : half + 1, columns] = lax.fori_loop(
                0, t // 64, part, jnp.zeros((1, 256), F32)
            )
            store_blocks(dw, dot(n2t[...], gp[:, columns]), whose, meta, pl.multiple_of(j * 256, 256), 256)
            store_blocks(
                dw, dot(gyt[...], hid[:, columns]), whose, meta, pl.multiple_of(CHUNK + j * 256, 256), 256
            )
            return carry

        lax.fori_loop(0, CHUNK // 256, tile, 0)

        def wide(j, carry):
            columns = pl.ds(pl.multiple_of(j * 256, 256), 256)
            a = dot_t(hid[...], wd[half, columns, :])
            b = dot_t(gp[...], wu[half, columns, :])
            if half == 1:
                a, b = a + out[:, columns], b + gn[:, columns]
            elif not first:
                a, b = a + out_in[:, columns], b + gn_in[:, columns]
            out[:, columns] = a
            gn[:, columns] = b
            return carry

        lax.fori_loop(0, C // 256, wide, 0)


def feed(offs, meta, n2, n2t, gy, gyt, bu, own, par, carried):
    t = n2.shape[0]
    first = carried is None
    carried = () if first else carried
    return pl.pallas_call(
        functools.partial(feed_kernel, offs, first),
        grid_spec=pltpu.PrefetchScalarGridSpec(
            num_scalar_prefetch=1,
            grid=(1,),
            in_specs=[
                whole((t, C)),
                whole((C, t)),
                whole((t, C)),
                whole((C, t)),
                whole((2, CHUNK)),
                *anywhere(8),
                *[whole((t, C))] * len(carried),
            ],
            out_specs=[
                whole((4, BLOCKS // 4, ROWS, 2 * CHUNK)),
                whole((4, BLOCKS // 4, ROWS, 2 * CHUNK)),
                whole((t, C)),
                whole((t, C)),
                whole((2, CHUNK)),
            ],
            scratch_shapes=[
                pltpu.VMEM((2, C, CHUNK), BF),
                pltpu.VMEM((2, C, CHUNK), BF),
                pltpu.VMEM((t, 256), F32),
                pltpu.VMEM((t, 256), F32),
                pltpu.VMEM((t, CHUNK), BF),
                pltpu.VMEM((t, CHUNK), BF),
                pltpu.SemaphoreType.DMA((2,)),
            ],
        ),
        out_shape=[
            jax.ShapeDtypeStruct((4, BLOCKS // 4, ROWS, 2 * CHUNK), BF),
            jax.ShapeDtypeStruct((4, BLOCKS // 4, ROWS, 2 * CHUNK), BF),
            jax.ShapeDtypeStruct((t, C), F32),
            jax.ShapeDtypeStruct((t, C), F32),
            jax.ShapeDtypeStruct((2, CHUNK), F32),
        ],
        name="feed",
        **params(12 * 10**9, 25 * 2**20),
    )(meta, n2, n2t, gy, gyt, bu, *own, *par, *carried)


def middle_back_kernel(off, meta, middle, out, gn, gy, att_own, att_par, b_down, gain, *refs):
    own, par = refs[:4], refs[4:8]
    output, gmid, gatt_own, gatt_par, dwo_own, dwo_par, sums = refs[8:15]
    w_own, w_par, gb, gbt, sem = refs[15:]
    columns = pl.ds(off, HALF)
    copies = piece_copies(own, meta[2], meta, columns, w_own, sem)
    copies += piece_copies(par, 1 - meta[2], meta, columns, w_par, sem)
    for copy in copies:
        copy.start()
    images = output.shape[0]
    sums[...] = jnp.zeros_like(sums)
    for copy in copies:
        copy.wait()
    for i in range(images):
        rows = pl.ds(i * NAT, NAT)
        value = middle[rows, :]
        output[i] = (value + (out[rows, :] + b_down[...]))[:TOK_IMG].astype(BF)
        hat, inverse = norm_stats(value)
        g = gn[rows, :]
        sums[0:1, :] += jnp.sum(g * hat, axis=0, keepdims=True)
        sums[1:2, :] += jnp.sum(g, axis=0, keepdims=True)
        total = gy[rows, :].astype(F32) + norm_back(g, hat, inverse, gain[...])
        gmid[rows, :] = total
        low = total.astype(BF)
        gb[rows, :] = low
        sums[2:3, :] += jnp.sum(low.astype(F32), axis=0, keepdims=True)
    transpose_into(gbt, gb)
    gatt_own[...] = dot(gb[...], w_own[...]).astype(BF)
    gatt_par[...] = dot(gb[...], w_par[...]).astype(BF)
    store_blocks(dwo_own, dot(gbt[...], att_own[...]), meta[2], meta, 0, HALF)
    store_blocks(dwo_par, dot(gbt[...], att_par[...]), 1 - meta[2], meta, 0, HALF)


def middle_back(off, meta, middle, out, gn, gy, att_own, att_par, b_down, gain, own, par):
    t = middle.shape[0]
    images = t // NAT
    slots = (4, BLOCKS // 4, ROWS, HALF)
    return pl.pallas_call(
        functools.partial(middle_back_kernel, off),
        grid_spec=pltpu.PrefetchScalarGridSpec(
            num_scalar_prefetch=1,
            grid=(1,),
            in_specs=[
                whole((t, C)),
                whole((t, C)),
                whole((t, C)),
                whole((t, C)),
                whole((t, HALF)),
                whole((t, HALF)),
                whole((1, C)),
                whole((1, C)),
                *anywhere(8),
            ],
            out_specs=[
                whole((images, TOK_IMG, C)),
                whole((t, C)),
                whole((t, HALF)),
                whole((t, HALF)),
                whole(slots),
                whole(slots),
                whole((8, C)),
            ],
            scratch_shapes=[
                pltpu.VMEM((C, HALF), BF),
                pltpu.VMEM((C, HALF), BF),
                pltpu.VMEM((t, C), BF),
                pltpu.VMEM((C, t), BF),
                pltpu.SemaphoreType.DMA,
            ],
        ),
        out_shape=[
            jax.ShapeDtypeStruct((images, TOK_IMG, C), BF),
            jax.ShapeDtypeStruct((t, C), F32),
            jax.ShapeDtypeStruct((t, HALF), BF),
            jax.ShapeDtypeStruct((t, HALF), BF),
            jax.ShapeDtypeStruct(slots, BF),
            jax.ShapeDtypeStruct(slots, BF),
            jax.ShapeDtypeStruct((8, C), F32),
        ],
        name="middle_back",
        **params(3 * 10**9, 18 * 2**20),
    )(meta, middle, out, gn, gy, att_own, att_par, b_down, gain, *own, *par)


def attend_back_kernel(meta, n1t, qkv, probs, gatt, dwo, lanes, to_window, to_nat, *refs):
    pieces = refs[:4]
    dw, gn1, pair, gbias, weight, gm, sem = refs[4:]
    i = pl.program_id(0)
    copies = piece_copies(pieces, meta[2], meta, pl.ds(0, 3 * HALF), weight, sem)

    @pl.when(i == 0)
    def _():
        for copy in copies:
            copy.start()
        pair[...] = jnp.zeros_like(pair)
        gbias[...] = jnp.zeros_like(gbias)
        dw[:, :, :, 3 * HALF :] = dwo[...]

    eye = unit_matrix(128)
    total = [jnp.zeros((NAT, HALF), F32) for _ in range(3)]
    for p in range(2):
        rows = pl.ds(pl.multiple_of((i * 2 + p) * PAIR, 16), PAIR)
        ga_all = dot(to_window[p], gatt[...]).astype(BF)
        gq, gk, gv = [], [], []
        for u in range(UNITS):
            q = qkv[rows, u * 128 : (u + 1) * 128]
            k = qkv[rows, HALF + u * 128 : HALF + (u + 1) * 128]
            v = qkv[rows, 2 * HALF + u * 128 : 2 * HALF + (u + 1) * 128]
            ga = ga_all[:, u * 128 : (u + 1) * 128]
            low = probs[p, u]
            stacked = jnp.concatenate([v * lanes[h : h + 1, :] for h in range(4)], axis=0)
            gprob = dot_t(stacked, ga).reshape(4, PAIR, PAIR)
            prob = low.astype(F32).reshape(4, PAIR, PAIR)
            row = jnp.sum(prob * gprob, axis=1, keepdims=True)
            gs = (prob * (gprob - row)).reshape(4 * PAIR, PAIR).astype(BF)
            pair[u] += gs.astype(F32)
            value = dot(low, ga)
            key = dot(gs, q)
            gv_u = jnp.zeros((PAIR, 128), F32)
            gk_u = jnp.zeros((PAIR, 128), F32)
            kt = dot_t(eye, k).astype(BF)
            for h in range(4):
                keep = lanes[h : h + 1, :].astype(F32)
                gv_u += value[h * PAIR : (h + 1) * PAIR] * keep
                gk_u += key[h * PAIR : (h + 1) * PAIR] * keep
                part = dot(kt[h * 32 : (h + 1) * 32], gs[h * PAIR : (h + 1) * PAIR])
                gq.append((part * HEAD_DIM**-0.5).astype(BF))
            gk.append(gk_u.astype(BF))
            gv.append(gv_u.astype(BF))
        total[0] = total[0] + dot_t(to_nat[p], jnp.concatenate(gq, axis=0))
        total[1] = total[1] + dot(to_nat[p], jnp.concatenate(gk, axis=1))
        total[2] = total[2] + dot(to_nat[p], jnp.concatenate(gv, axis=1))
    here = pl.ds(pl.multiple_of(i * NAT, 16), NAT)
    for n in range(3):
        gm[here, n * HALF : (n + 1) * HALF] = total[n].astype(BF)
        gbias[0:1, n * HALF : (n + 1) * HALF] += jnp.sum(total[n], axis=0, keepdims=True)

    @pl.when(i == pl.num_programs(0) - 1)
    def _():
        def step(j, carry):
            column = pl.multiple_of(j * HALF, 128)
            value = dot(n1t[...], gm[:, pl.ds(column, HALF)])
            store_blocks(dw, value, meta[2], meta, column, HALF)
            return carry

        lax.fori_loop(0, 3, step, 0)
        for copy in copies:
            copy.wait()

        def wide(j, carry):
            columns = pl.ds(pl.multiple_of(j * 256, 256), 256)
            gn1[:, columns] = dot_t(gm[...], weight[columns, :])
            return carry

        lax.fori_loop(0, C // 256, wide, 0)


def attend_back(meta, n1t, qkv, probs, gatt, dwo, lanes, to_window, to_nat, pieces):
    t = gatt.shape[0]
    images = t // NAT
    tw = images * 2 * PAIR
    slots = (4, BLOCKS // 4, ROWS)
    return pl.pallas_call(
        attend_back_kernel,
        grid_spec=pltpu.PrefetchScalarGridSpec(
            num_scalar_prefetch=1,
            grid=(images,),
            in_specs=[
                whole((C, t)),
                whole((tw, 3 * HALF)),
                pl.BlockSpec((2, UNITS, 4 * PAIR, PAIR), lambda i, m: (i, 0, 0, 0)),
                pl.BlockSpec((NAT, HALF), lambda i, m: (i, 0)),
                whole((*slots, HALF)),
                whole((8, 128)),
                whole((2, PAIR, NAT)),
                whole((2, NAT, PAIR)),
                *anywhere(4),
            ],
            out_specs=[
                whole((*slots, 4 * HALF)),
                whole((t, C)),
                whole((UNITS, 4 * PAIR, PAIR)),
                whole((8, 3 * HALF)),
            ],
            scratch_shapes=[
                pltpu.VMEM((C, 3 * HALF), BF),
                pltpu.VMEM((t, 3 * HALF), BF),
                pltpu.SemaphoreType.DMA,
            ],
        ),
        out_shape=[
            jax.ShapeDtypeStruct((*slots, 4 * HALF), BF),
            jax.ShapeDtypeStruct((t, C), F32),
            jax.ShapeDtypeStruct((UNITS, 4 * PAIR, PAIR), F32),
            jax.ShapeDtypeStruct((8, 3 * HALF), F32),
        ],
        name="attend_back",
        **params(6 * 10**9, 16 * 2**20),
    )(meta, n1t, qkv, probs, gatt, dwo, lanes, to_window, to_nat, *pieces)


def epilogue_kernel(x, gmid, gn_a, gn_b, gain, grad, sums):
    i = pl.program_id(0)
    hat, inverse = norm_stats(x[...].astype(F32))
    g = gn_a[...] + gn_b[...]
    total = gmid[...] + norm_back(g, hat, inverse, gain[...])
    grad[0] = total[:TOK_IMG]

    @pl.when(i == 0)
    def _():
        sums[...] = jnp.zeros_like(sums)

    sums[0:1, :] += jnp.sum(g * hat, axis=0, keepdims=True)
    sums[1:2, :] += jnp.sum(g, axis=0, keepdims=True)


def epilogue(x, gmid, gn_a, gn_b, gain):
    images = x.shape[0] // NAT
    block = pl.BlockSpec((NAT, C), lambda i: (i, 0))
    return pl.pallas_call(
        epilogue_kernel,
        grid=(images,),
        in_specs=[block] * 4 + [whole((1, C))],
        out_specs=[pl.BlockSpec((1, TOK_IMG, C), lambda i: (i, 0, 0)), whole((8, C))],
        out_shape=[
            jax.ShapeDtypeStruct((images, TOK_IMG, C), F32),
            jax.ShapeDtypeStruct((8, C), F32),
        ],
        name="epilogue",
        **params(10**8, 12 * 2**20),
    )(x, gmid, gn_a, gn_b, gain)


def window_tables():
    move = np.zeros((2, PAIR, NAT), np.float32)
    token = np.zeros((2, 2 * WIN * WIN), np.int32)
    for p in range(2):
        for r in range(2 * WIN * WIN):
            right, cell = r // (WIN * WIN), r % (WIN * WIN)
            row = (p * WIN + cell // WIN + SHIFT) % SIDE
            column = (right * WIN + cell % WIN + SHIFT) % SIDE
            token[p, r] = row * SIDE + column
            move[p, r, token[p, r]] = 1.0
    return move, move.transpose(0, 2, 1).copy()


def to_windows(tokens):
    images = tokens.shape[0]
    lattice = jnp.roll(tokens.reshape(images, SIDE, SIDE), (-SHIFT, -SHIFT), axis=(1, 2))
    lattice = lattice.reshape(images, 2, WIN, 2, WIN)
    return jnp.moveaxis(lattice, 3, 2).reshape(images * 2, 2 * WIN * WIN)


def body(
    n_dp,
    inputs,
    region,
    rel_index,
    w_qkv,
    w_out,
    w_up,
    w_down,
    b_qv,
    bias_table,
    b_out,
    b_up,
    b_down,
    gain_one,
    shift_one,
    gain_two,
    shift_two,
    cotangent,
):
    highest = lax.Precision.HIGHEST
    dp, core = lax.axis_index("dp"), lax.axis_index("tensor")
    other = 1 - core
    images = inputs.shape[0]
    rows = w_out.shape[0]
    if staged(n_dp):
        yx, z, here = dp % 4, dp // 4, core
    else:
        yx, z, here = 0 * dp, 0 * dp, core
    meta = jnp.stack([yx, z, core]).astype(jnp.int32)
    meta_par = jnp.stack([yx, z, other]).astype(jnp.int32)

    def pick(own, par):
        return jnp.where(core == 0, jnp.concatenate([own, par]), jnp.concatenate([par, own]))

    own_a, par_a = gather_pieces(w_qkv.reshape(rows, -1), n_dp)
    own_b, par_b = gather_pieces(
        jnp.concatenate([w_out, w_up[:, :CHUNK], w_down[:, :CHUNK]], axis=1), n_dp
    )
    own_c, par_c = gather_pieces(
        jnp.concatenate([w_up[:, CHUNK:], w_down[:, CHUNK:]], axis=1), n_dp
    )

    move, back = window_tables()
    to_window, to_nat = jnp.asarray(move, BF), jnp.asarray(back, BF)
    lane_head = np.zeros((8, 128), np.float32)
    for h in range(4):
        lane_head[h, h * HEAD_DIM : (h + 1) * HEAD_DIM] = 1.0
    lanes = jnp.asarray(lane_head, BF)

    cells = WIN * WIN
    offsets = lax.broadcasted_iota(jnp.int32, (cells * cells, TABLE), 1)
    onehot = (rel_index.T.reshape(-1, 1) == offsets).astype(F32)
    near = jnp.dot(onehot, bias_table, precision=highest).T.reshape(HEADS, cells, cells)
    bias = jnp.full((HEADS, PAIR, PAIR), FAR, F32)
    bias = bias.at[:, :cells, :cells].set(near)
    bias = bias.at[:, cells : 2 * cells, cells : 2 * cells].set(near)
    bias = bias.reshape(HEADS // 4, 4 * PAIR, PAIR)
    labels = to_windows(lax.dynamic_slice_in_dim(region, core * images, images, 0))
    labels = jnp.pad(labels, ((0, 0), (0, PAIR - 2 * cells)))
    regm = jnp.where(labels[:, :, None] == labels[:, None, :], 0.0, -100.0).astype(F32)

    pad = ((0, 0), (0, NAT - TOK_IMG), (0, 0))
    x = jnp.pad(inputs, pad).reshape(images * NAT, C)
    gy = jnp.pad(cotangent, pad).reshape(images * NAT, C)

    def row(v):
        return v.reshape(1, -1)

    scale = np.ones((1, 3 * HALF), np.float32)
    scale[:, :HALF] = HEAD_DIM**-0.5
    scale_row = jnp.asarray(scale)

    def bias_of(half):
        part = lax.dynamic_slice_in_dim(b_qv, half * HALF, HALF, 1)
        return jnp.concatenate([part[0], jnp.zeros((HALF,), F32), part[1]]).reshape(1, -1)

    n1, n1w, n1t, gyt, gbd = prologue(x, gy, row(gain_one), row(shift_one), to_window)
    att_own, qkv_own, prob_own = attend(
        meta, n1w, bias_of(core), scale_row, bias, regm, lanes, to_nat, own_a
    )
    att_par, qkv_par, prob_par = attend(
        meta_par, n1w, bias_of(other), scale_row, bias, regm, lanes, to_nat, par_a
    )
    middle, n2, n2t = middle_forward(
        0, meta, x, att_own, att_par, row(b_out), row(gain_two), row(shift_two), own_b, par_b
    )

    def up_bias(chunk):
        halves = [
            lax.dynamic_slice_in_dim(b_up, half * (FF // 2) + chunk * CHUNK, CHUNK, 0)
            for half in (other, core)
        ]
        return jnp.stack(halves)

    dw_own_b, dw_par_b, out, gn, gbu_b = feed(
        (HALF, HALF + CHUNK), meta, n2, n2t, gy, gyt, up_bias(0), own_b, par_b, None
    )
    dw_own_c, dw_par_c, out, gn, gbu_c = feed(
        (0, CHUNK), meta, n2, n2t, gy, gyt, up_bias(1), own_c, par_c, (out, gn)
    )
    output, gmid, gatt_own, gatt_par, dwo_own, dwo_par, sums_two = middle_back(
        0, meta, middle, out, gn, gy, att_own, att_par, row(b_down), row(gain_two), own_b, par_b
    )
    dw_par_a, gn_par, pair_par, gb_par = attend_back(
        meta_par, n1t, qkv_par, prob_par, gatt_par, dwo_par, lanes, to_window, to_nat, par_a
    )
    dw_own_a, gn_own, pair_own, gb_own = attend_back(
        meta, n1t, qkv_own, prob_own, gatt_own, dwo_own, lanes, to_window, to_nat, own_a
    )
    grad_inputs, sums_one = epilogue(x, gmid, gn_own, gn_par, row(gain_one))

    part_b = reduce_blocks(dw_own_b, dw_par_b, n_dp)
    part_c = reduce_blocks(dw_own_c, dw_par_c, n_dp)
    part_a = reduce_blocks(dw_own_a, dw_par_a, n_dp)
    shard_up = jnp.concatenate([part_b[:, :CHUNK], part_c[:, :CHUNK]], axis=1)
    shard_down = jnp.concatenate([part_b[:, CHUNK:], part_c[:, CHUNK:]], axis=1)
    shard_qkv = part_a[:, : 3 * HALF].reshape(rows, 3, HALF)
    shard_out = part_a[:, 3 * HALF :]

    pair = pick(pair_own, pair_par).reshape(HEADS, PAIR, PAIR)
    pair = pair[:, :cells, :cells] + pair[:, cells : 2 * cells, cells : 2 * cells]
    table = jnp.dot(onehot.T, pair.reshape(HEADS, -1).T, precision=highest)
    bias_qv = jnp.stack(
        [
            pick(gb_own[0, :HALF], gb_par[0, :HALF]),
            pick(gb_own[0, 2 * HALF :], gb_par[0, 2 * HALF :]),
        ]
    )
    bias_up = pick(
        jnp.concatenate([gbu_b[1], gbu_c[1]]), jnp.concatenate([gbu_b[0], gbu_c[0]])
    )
    small = (
        bias_qv,
        table,
        sums_two[2],
        bias_up,
        gbd[0],
        sums_one[0],
        sums_one[1],
        sums_two[0],
        sums_two[1],
    )
    flat = jnp.concatenate([v.reshape(-1) for v in small])
    fill = -flat.shape[0] % 1024
    flat = sum_everywhere(jnp.pad(flat, (0, fill)).reshape(-1, 128), n_dp).reshape(-1)
    summed, start = [], 0
    for v in small:
        summed.append(flat[start : start + v.size].reshape(v.shape))
        start += v.size
    return (output, grad_inputs, shard_qkv, shard_out, shard_up, shard_down, *summed)


def solution(mesh):
    placed = (
        P(("dp", "tensor"), None, None),
        P("dp", None),
        P(),
        P("dp", None, "tensor"),
        P("dp", "tensor"),
        P("dp", "tensor"),
        P("dp", "tensor"),
        P(),
        P(),
        P(),
        P(),
        P(),
        P(),
        P(),
        P(),
        P(),
        P(("dp", "tensor"), None, None),
    )
    return jax.shard_map(
        functools.partial(body, mesh.shape["dp"]),
        mesh=mesh,
        in_specs=placed,
        out_specs=(
            P(("dp", "tensor"), None, None),
            P(("dp", "tensor"), None, None),
            P("dp", None, "tensor"),
            P("dp", "tensor"),
            P("dp", "tensor"),
            P("dp", "tensor"),
            P(),
            P(),
            P(),
            P(),
            P(),
            P(),
            P(),
            P(),
            P(),
        ),
        check_vma=False,
    )
```
